32 devices in a mesh: dp: 8 (over z, y), tensor: 4 (over x, core).
Axes of the slice: x: 2, y: 2, z: 4, core: 2. Of those that a mesh axis runs over, the one named last changes fastest.
Arguments:
- layer_in: bfloat16 [16384, 768], P(('dp', 'tensor')), may hold values from -6 to 6
- ln1_gain: bfloat16 [768], P('dp'), may hold values from 0.5 to 1.5
- ln1_bias: bfloat16 [768], P('dp'), may hold values from -1.75 to 1.75
- query_weight: bfloat16 [768, 768], P('dp', 'tensor'), may hold values from -0.4375 to 0.4375
- query_bias: bfloat16 [768], P(('tensor', 'dp')), may hold values from -1.75 to 1.75
- key_weight: bfloat16 [768, 768], P('dp', 'tensor'), may hold values from -0.21875 to 0.21875
- value_weight: bfloat16 [768, 768], P('dp', 'tensor'), may hold values from -0.21875 to 0.21875
- value_bias: bfloat16 [768], P(('tensor', 'dp')), may hold values from -1.75 to 1.75
- inner_gain: bfloat16 [768], P(('tensor', 'dp')), may hold values from 0.5 to 1.5
- inner_bias: bfloat16 [768], P(('tensor', 'dp')), may hold values from -1.75 to 1.75
- output_weight: bfloat16 [768, 768], P('tensor', 'dp'), may hold values from -0.21875 to 0.21875
- output_bias: bfloat16 [768], P('dp'), may hold values from -1.75 to 1.75
- ln2_gain: bfloat16 [768], P('dp'), may hold values from 0.5 to 1.5
- ln2_bias: bfloat16 [768], P('dp'), may hold values from -1.75 to 1.75
- up_weight: bfloat16 [768, 3072], P('dp', 'tensor'), may hold values from -0.21875 to 0.21875
- up_bias: bfloat16 [3072], P(('tensor', 'dp')), may hold values from -1.75 to 1.75
- outer_gain: bfloat16 [3072], P(('tensor', 'dp')), may hold values from 0.5 to 1.5
- outer_bias: bfloat16 [3072], P(('tensor', 'dp')), may hold values from -1.75 to 1.75
- down_weight: bfloat16 [3072, 768], P('tensor', 'dp'), may hold values from -0.109375 to 0.109375
- down_bias: bfloat16 [768], P('dp'), may hold values from -1.75 to 1.75
- out_grad: bfloat16 [16384, 768], P(('dp', 'tensor')), may hold values from -12 to 12
- prefix: int32 [4], replicated, may hold values from 2560 to 3584, as said below
Outputs:
- layer_out: bfloat16 [16384, 768], P(('dp', 'tensor'))
- input_grad: float32 [16384, 768], P(('dp', 'tensor'))
- grad_ln1_gain: float32 [768], P('dp')
- grad_ln1_bias: float32 [768], P('dp')
- grad_query_weight: float32 [768, 768], P('dp', 'tensor')
- grad_query_bias: float32 [768], P(('tensor', 'dp'))
- grad_key_weight: float32 [768, 768], P('dp', 'tensor')
- grad_value_weight: float32 [768, 768], P('dp', 'tensor')
- grad_value_bias: float32 [768], P(('tensor', 'dp'))
- grad_inner_gain: float32 [768], P(('tensor', 'dp'))
- grad_inner_bias: float32 [768], P(('tensor', 'dp'))
- grad_output_weight: float32 [768, 768], P('tensor', 'dp')
- grad_output_bias: float32 [768], P('dp')
- grad_ln2_gain: float32 [768], P('dp')
- grad_ln2_bias: float32 [768], P('dp')
- grad_up_weight: float32 [768, 3072], P('dp', 'tensor')
- grad_up_bias: float32 [3072], P(('tensor', 'dp'))
- grad_outer_gain: float32 [3072], P(('tensor', 'dp'))
- grad_outer_bias: float32 [3072], P(('tensor', 'dp'))
- grad_down_weight: float32 [3072, 768], P('tensor', 'dp')
- grad_down_bias: float32 [768], P('dp')
The draws below stay inside these ranges and needn't reach their ends.
Inputs may be any that keep to these rules, and one draw needn't show every extreme that they name: prefix[s] is the number of leading positions of sequence s that attend both ways; it reaches past the first 2048 positions in every sequence, and some sequence has exactly 3584.
All inputs are finite; a program needn't handle non-finite values.
Results may differ from the reference program's by a relative error of at most 0.017.
Values may be sent and summed in bfloat16 or wider, within the bound.
No kernel may reach another device: no remote copies, remote signals or barrier semaphores. Data moves between devices by JAX's collectives and lax.ppermute only.
A program may use at most 192 MiB of HBM per device.

```python
from functools import partial
import jax
import jax.numpy as jnp
from jax import lax

D = 768
H = 12
DH = 64
FF = 3072
SEG1 = 2048
SEG2 = 4096
HD = 768
N_SEQ = 4
TOKENS = 16384


def draw_prefix(key, part):
    first_key = jax.random.fold_in(key, 11)
    pick_key = jax.random.fold_in(key, 12)
    top_len = SEG2 - SEG1 // 4
    lengths = jax.random.randint(first_key, (N_SEQ,), SEG1 + SEG1 // 4, top_len + 1)
    chosen = jax.random.randint(pick_key, (), 0, N_SEQ)
    return jnp.where(jnp.arange(N_SEQ) == chosen, top_len, lengths).astype(jnp.int32)


def spiked(result, own_key, source, target, parts, factor):
    owner, partner = [(jnp.arange(result.shape[dim]) // (result.shape[dim] // parts)).reshape([-1 if axis == dim else 1 for axis in range(result.ndim)]) for dim in (source, target)]
    chosen = jax.random.permutation(own_key, parts)[partner]
    strong = (owner == chosen) | (owner == (partner + parts // 2) % parts)
    return jnp.where(strong, factor * result, result)


def block_scale(key, extent, split, least, top_value):
    factor_of, own = 1.0, jax.random.fold_in(key, 6)
    for dim, blocks in split:
        steps = jnp.exp(jax.random.uniform(jax.random.fold_in(own, dim), (blocks,), jnp.float32, least / len(split), top_value / len(split)))
        factor_of = factor_of * jnp.repeat(steps, extent[dim] // blocks).reshape([-1 if axis == dim else 1 for axis in range(len(extent))])
    return factor_of


def bell_draw(key, dims, width, reach, pieces=(), kind=jnp.bfloat16):
    result = jax.random.normal(key, dims, jnp.float32) * width
    if len(pieces) > 0:
        result = block_scale(key, dims, pieces, -0.22, 0.18) * result
    return jnp.clip(result, min=-reach, max=reach).astype(kind)


def gaussian_with(rng, dims, width, limit, split, heavy, kind=jnp.bfloat16):
    result = width * jax.random.normal(rng, dims, jnp.float32)
    if split:
        result = result * block_scale(rng, dims, split, -0.22, 0.18)
    return jnp.clip(spiked(result, jax.random.fold_in(rng, 3), *heavy), -limit, limit).astype(kind)


def setup_inputs(seed: int = 0) -> dict:
    keys = jax.random.split(jax.random.key(seed), 23)
    return {
        "layer_in": bell_draw(keys[0], (TOKENS, D), 1.0, 6.0, ((0, 32),)),
        "ln1_gain": jnp.clip(1.0 + 0.1 * jax.random.normal(keys[1], (D,), jnp.float32), 0.5, 1.5).astype(jnp.bfloat16),
        "ln1_bias": bell_draw(keys[2], (D,), 0.3, 1.75, ((0, 8),)),
        "query_weight": bell_draw(keys[3], (D, HD), (D // 4) ** -0.5, 0.4375, ((0, 8), (1, 4))),
        "query_bias": bell_draw(keys[4], (HD,), 0.3, 1.75, ((0, 32),)),
        "key_weight": bell_draw(keys[5], (D, HD), D ** -0.5, 0.21875, ((0, 8), (1, 4))),
        "value_weight": bell_draw(keys[6], (D, HD), D ** -0.5, 0.21875, ((0, 8), (1, 4))),
        "value_bias": bell_draw(keys[7], (HD,), 0.3, 1.75, ((0, 32),)),
        "inner_gain": jnp.clip(1.0 + 0.1 * jax.random.normal(keys[8], (HD,), jnp.float32), 0.5, 1.5).astype(jnp.bfloat16),
        "inner_bias": bell_draw(keys[9], (HD,), 0.3, 1.75, ((0, 32),)),
        "output_weight": bell_draw(keys[10], (HD, D), HD ** -0.5, 0.21875, ((0, 4), (1, 8))),
        "output_bias": bell_draw(keys[11], (D,), 0.3, 1.75, ((0, 8),)),
        "ln2_gain": jnp.clip(1.0 + 0.1 * jax.random.normal(keys[12], (D,), jnp.float32), 0.5, 1.5).astype(jnp.bfloat16),
        "ln2_bias": bell_draw(keys[13], (D,), 0.3, 1.75, ((0, 8),)),
        "up_weight": bell_draw(keys[14], (D, FF), D ** -0.5, 0.21875, ((0, 8), (1, 4))),
        "up_bias": bell_draw(keys[15], (FF,), 0.3, 1.75, ((0, 32),)),
        "outer_gain": jnp.clip(1.0 + 0.1 * jax.random.normal(keys[16], (FF,), jnp.float32), 0.5, 1.5).astype(jnp.bfloat16),
        "outer_bias": bell_draw(keys[17], (FF,), 0.3, 1.75, ((0, 32),)),
        "down_weight": bell_draw(keys[18], (FF, D), FF ** -0.5, 0.109375, ((0, 4), (1, 8))),
        "down_bias": bell_draw(keys[19], (D,), 0.3, 1.75, ((0, 8),)),
        "out_grad": gaussian_with(keys[20], (TOKENS, D), 1.0, 12.0, ((0, 32),), (0, 1, 32, 2.75)),
        "prefix": draw_prefix(jax.random.fold_in(keys[22], 71), 0),
    }


@jax.custom_vjp
def low(v):
    return lax.optimization_barrier(v.astype(jnp.bfloat16)).astype(jnp.float32)

@jax.custom_vjp
def low_back(v):
    return v

def low_keep(v):
    return (low(v), None)

def low_pass(kept, grad):
    return (grad,)

def back_keep(v):
    return (v, None)

def back_low(kept, grad):
    return (low(grad),)
low.defvjp(low_keep, low_pass)
low_back.defvjp(back_keep, back_low)
epsilon = 1e-05
masked_score = -1000000000.0
score_scale = 0.125

def product(left_side, right_side):
    return jnp.dot(left_side, right_side, precision=lax.Precision.HIGHEST)

def norm_rows(values, norm_gain, norm_shift):
    middle_point = lax.optimization_barrier(jnp.mean(values, axis=-1, keepdims=True))
    spread = lax.optimization_barrier(jnp.mean(values * values, axis=-1, keepdims=True)) - middle_point * middle_point
    return (values - middle_point) * lax.rsqrt(spread + epsilon) * norm_gain + norm_shift

def attend(query_rows, key_rows, value_rows, query_pos, key_pos, prefix_len):
    scores = low_back(product(query_rows, key_rows.T) * score_scale)
    allowed = (key_pos[None, :] <= query_pos[:, None]) | (key_pos[None, :] < prefix_len)
    scores = jnp.where(allowed, scores, masked_score)
    log_total = jax.nn.logsumexp(scores, axis=1)
    attention_weights = jnp.exp(scores - log_total[:, None])
    return (low_back(product(low(attention_weights), value_rows)), log_total)

def head_sequence(query_rows, key_rows, value_rows, prefix_len, parity):
    positions = jnp.arange(SEG2, dtype=jnp.int32)
    split_pos = positions.reshape(2, SEG1)
    near_out, near_log = jax.vmap(attend, in_axes=(0, 0, 0, 0, 0, None))(query_rows.reshape(2, SEG1, DH), key_rows.reshape(2, SEG1, DH), value_rows.reshape(2, SEG1, DH), split_pos, split_pos, prefix_len)

    def dilate(row_block):
        paired = row_block.reshape(SEG1, 2, DH)
        return jnp.where(parity == 1, paired[:, 1], paired[:, 0])
    sparse_pos = 2 * jnp.arange(SEG1, dtype=jnp.int32) + parity
    far_out, far_log = attend(dilate(query_rows), dilate(key_rows), dilate(value_rows), sparse_pos, sparse_pos, prefix_len)
    near_pairs = near_out.reshape(SEG1, 2, DH)
    near_logs = near_log.reshape(SEG1, 2)
    slot_pick = jnp.arange(2, dtype=jnp.int32)[None, :] == parity
    row_top = jnp.where(slot_pick, jnp.maximum(near_logs, far_log[:, None]), near_logs)
    near_weight = jnp.exp(near_logs - row_top)
    far_weight = jnp.where(slot_pick, jnp.exp(jnp.where(slot_pick, far_log[:, None] - row_top, 0.0)), 0.0)
    row_total = near_weight + far_weight
    merged = (near_weight[:, :, None] * near_pairs + far_weight[:, :, None] * far_out[:, None, :]) / row_total[:, :, None]
    return merged.reshape(SEG2, DH)

def forward(prefix, layer_in, ln1_gain, ln1_bias, query_weight, query_bias, key_weight, value_weight, value_bias, inner_gain, inner_bias, output_weight, output_bias, ln2_gain, ln2_bias, up_weight, up_bias, outer_gain, outer_bias, down_weight, down_bias):
    hidden_one = low(norm_rows(layer_in, ln1_gain, ln1_bias))
    query_rows = low(low_back(product(hidden_one, query_weight) + query_bias))
    key_rows = low(low_back(product(hidden_one, key_weight)))
    value_rows = low(low_back(product(hidden_one, value_weight) + value_bias))

    def arrange(row_block):
        return row_block.reshape(N_SEQ, SEG2, H, DH).transpose(0, 2, 1, 3).reshape(N_SEQ * H, SEG2, DH)

    def per_member(member):
        return jax.checkpoint(head_sequence)(member[0], member[1], member[2], member[3], member[4])
    head_ids = jnp.arange(N_SEQ * H, dtype=jnp.int32) % H
    prefix_members = jnp.repeat(prefix, H)
    mixed = lax.map(per_member, (arrange(query_rows), arrange(key_rows), arrange(value_rows), prefix_members, head_ids % 2))
    attended = mixed.reshape(N_SEQ, H, SEG2, DH).transpose(0, 2, 1, 3).reshape(N_SEQ * SEG2, H * DH)
    inner_rows = low(norm_rows(attended, inner_gain, inner_bias))
    middle = layer_in + low_back(product(inner_rows, output_weight) + output_bias)
    hidden_two = low(norm_rows(middle, ln2_gain, ln2_bias))
    up_rows = low_back(product(hidden_two, up_weight) + up_bias)
    outer_rows = low(norm_rows(jax.nn.gelu(up_rows, approximate=False), outer_gain, outer_bias))
    return middle + low_back(product(outer_rows, down_weight) + down_bias)

def reference(layer_in, ln1_gain, ln1_bias, query_weight, query_bias, key_weight, value_weight, value_bias, inner_gain, inner_bias, output_weight, output_bias, ln2_gain, ln2_bias, up_weight, up_bias, outer_gain, outer_bias, down_weight, down_bias, out_grad, prefix):
    floats = (layer_in.astype(jnp.float32), ln1_gain.astype(jnp.float32), ln1_bias.astype(jnp.float32), query_weight.astype(jnp.float32), query_bias.astype(jnp.float32), key_weight.astype(jnp.float32), value_weight.astype(jnp.float32), value_bias.astype(jnp.float32), inner_gain.astype(jnp.float32), inner_bias.astype(jnp.float32), output_weight.astype(jnp.float32), output_bias.astype(jnp.float32), ln2_gain.astype(jnp.float32), ln2_bias.astype(jnp.float32), up_weight.astype(jnp.float32), up_bias.astype(jnp.float32), outer_gain.astype(jnp.float32), outer_bias.astype(jnp.float32), down_weight.astype(jnp.float32), down_bias.astype(jnp.float32))
    output, pull_back = jax.vjp(partial(forward, prefix), *floats)
    gradients = pull_back(out_grad.astype(jnp.float32))
    return (output.astype(jnp.bfloat16), gradients[0], gradients[1], gradients[2], gradients[3], gradients[4], gradients[5], gradients[6], gradients[7], gradients[8], gradients[9], gradients[10], gradients[11], gradients[12], gradients[13], gradients[14], gradients[15], gradients[16], gradients[17], gradients[18], gradients[19])
```

```python
import math
from functools import partial

import jax
import jax.numpy as jnp
from jax import lax
from jax.experimental import pallas as pl
from jax.experimental.pallas import tpu as pltpu
from jax.sharding import PartitionSpec as P

epsilon = 1e-05
score_scale = 0.125
LOG2 = math.log(2.0)
CLOSED = -1e9
QB = 512


def mm(a, b):
    return jnp.dot(a, b, preferred_element_type=jnp.float32)


def flip(value):
    return value.astype(jnp.float32).T.astype(value.dtype)


def block_base(scal, base, rel, parity):
    return base + ((scal[0] ^ rel) << 9) + parity


def query_limit(scal, qb):
    lane = lax.broadcasted_iota(jnp.int32, (1, QB), 1)
    parity = qb // 2
    rel = (qb % 2) * 2
    low = block_base(scal, scal[1], rel, parity)
    high = block_base(scal, scal[1], rel + 1, parity)
    pos = 2 * (lane & 255) + jnp.where(lane < 256, low, high)
    return jnp.maximum(pos, scal[2] - 1)


def shut(s, scal, base, chunk, parity, limit):
    row = 2 * lax.broadcasted_iota(jnp.int32, (256, QB), 0)
    parts = []
    for sub in range(2):
        room = limit - block_base(scal, base, 2 * chunk + sub, parity)
        parts.append(jnp.where(row <= room, s[sub * 256 : sub * 256 + 256], CLOSED))
    return jnp.concatenate(parts, axis=0)


def near_fwd_kernel(scal, q_ref, k_ref, v_ref, o_ref, l_ref, k_nat, v_aug):
    head, qb = pl.program_id(0), pl.program_id(1)
    par = scal[4 + head]

    @pl.when(qb == 0)
    def _():
        k_nat[...] = flip(k_ref[...])
        v_aug[0:64] = v_ref[...]
        v_aug[64:80] = jnp.ones((16, 2048), jnp.bfloat16)

    far = qb // 2 == par

    def body(masked):
        q = q_ref[...]
        limit = query_limit(scal, qb)
        top = acc = None
        for c in range(4):
            s = mm(k_nat[c * 512 : c * 512 + 512], q)
            if masked:
                s = shut(s, scal, scal[1], c % 2, c // 2, limit)
            twice = jnp.where(far & (par == c // 2), LOG2, 0.0)
            peak = jnp.max(s, axis=0, keepdims=True)
            new = peak if c == 0 else jnp.maximum(top, peak)
            p = jnp.exp(s - (new - twice)).astype(jnp.bfloat16)
            part = mm(v_aug[:, c * 512 : c * 512 + 512], p)
            acc = part if c == 0 else acc * jnp.exp(top - new) + part
            top = new
        total = acc[64:65]
        o_ref[...] = acc[0:64] / total
        l_ref[0] = top + jnp.log(total)

    need = scal[2] < scal[1] + 2048
    pl.when(need)(lambda: body(True))
    pl.when(jnp.logical_not(need))(lambda: body(False))


def near_fwd(scal, q, k, v):
    return pl.pallas_call(
        near_fwd_kernel,
        grid_spec=pltpu.PrefetchScalarGridSpec(
            num_scalar_prefetch=1,
            grid=(3, 4),
            in_specs=[
                pl.BlockSpec((64, QB), lambda h, i, s: (h, i)),
                pl.BlockSpec((64, 2048), lambda h, i, s: (h, 0)),
                pl.BlockSpec((64, 2048), lambda h, i, s: (h, 0)),
            ],
            out_specs=[
                pl.BlockSpec((64, QB), lambda h, i, s: (h, i)),
                pl.BlockSpec((1, 1, QB), lambda h, i, s: (h, 0, i)),
            ],
            scratch_shapes=[
                pltpu.VMEM((2048, 64), jnp.bfloat16),
                pltpu.VMEM((80, 2048), jnp.bfloat16),
            ],
        ),
        out_shape=[
            jax.ShapeDtypeStruct((192, 2048), jnp.float32),
            jax.ShapeDtypeStruct((3, 1, 2048), jnp.float32),
        ],
        cost_estimate=pl.CostEstimate(flops=13000000000, bytes_accessed=4000000, transcendentals=12582912),
        name="near_fwd",
    )(scal, q, k, v)


def cross_fwd_kernel(scal, q_ref, k_ref, v_ref, o1_ref, l1_ref, o_ref, l_ref, k_nat, v_aug):
    head, qb = pl.program_id(0), pl.program_id(1)
    par = scal[4 + head]
    far = qb // 2 == par

    @pl.when(qb == 0)
    def _():
        k_nat[...] = flip(k_ref[...])
        v_aug[0:64] = v_ref[...]
        v_aug[64:80] = jnp.ones((16, 1024), jnp.bfloat16)

    @pl.when(jnp.logical_not(far))
    def _():
        o_ref[...] = o1_ref[...].astype(jnp.bfloat16)
        l_ref[...] = l1_ref[...]

    def body(masked):
        q = q_ref[...]
        limit = query_limit(scal, qb)
        top = acc = None
        for c in range(2):
            s = mm(k_nat[c * 512 : c * 512 + 512], q)
            if masked:
                s = shut(s, scal, scal[3], c, par, limit)
            peak = jnp.max(s, axis=0, keepdims=True)
            new = peak if c == 0 else jnp.maximum(top, peak)
            p = jnp.exp(s - new).astype(jnp.bfloat16)
            part = mm(v_aug[:, c * 512 : c * 512 + 512], p)
            acc = part if c == 0 else acc * jnp.exp(top - new) + part
            top = new
        l1 = l1_ref[0]
        new = jnp.maximum(l1, top)
        w1 = jnp.exp(l1 - new)
        w2 = jnp.exp(top - new)
        total = w1 + w2 * acc[64:65]
        o_ref[...] = ((w1 * o1_ref[...] + w2 * acc[0:64]) / total).astype(jnp.bfloat16)
        l_ref[0] = new + jnp.log(total)

    need = scal[3] > scal[1]
    pl.when(far & need)(lambda: body(True))
    pl.when(far & jnp.logical_not(need))(lambda: body(False))


def cross_fwd(scal, q, k, v, o1, l1):
    return pl.pallas_call(
        cross_fwd_kernel,
        grid_spec=pltpu.PrefetchScalarGridSpec(
            num_scalar_prefetch=1,
            grid=(3, 4),
            in_specs=[
                pl.BlockSpec((64, QB), lambda h, i, s: (h, i)),
                pl.BlockSpec((64, 1024), lambda h, i, s: (h, 0)),
                pl.BlockSpec((64, 1024), lambda h, i, s: (h + 3, 0)),
                pl.BlockSpec((64, QB), lambda h, i, s: (h, i)),
                pl.BlockSpec((1, 1, QB), lambda h, i, s: (h, 0, i)),
            ],
            out_specs=[
                pl.BlockSpec((64, QB), lambda h, i, s: (h, i)),
                pl.BlockSpec((1, 1, QB), lambda h, i, s: (h, 0, i)),
            ],
            scratch_shapes=[
                pltpu.VMEM((1024, 64), jnp.bfloat16),
                pltpu.VMEM((80, 1024), jnp.bfloat16),
            ],
        ),
        out_shape=[
            jax.ShapeDtypeStruct((192, 2048), jnp.bfloat16),
            jax.ShapeDtypeStruct((3, 1, 2048), jnp.float32),
        ],
        cost_estimate=pl.CostEstimate(flops=3300000000, bytes_accessed=4000000, transcendentals=3145728),
        name="cross_fwd",
    )(scal, q, k, v, o1, l1)


def back_chunk(masked_fn, k_c, v_c, kT_c, q, q_nat, do, do_nat, shift, delta):
    s = mm(k_c, q)
    if masked_fn is not None:
        s = masked_fn(s)
    p = jnp.exp(s - shift)
    dp = mm(v_c, do)
    ds = (p * (dp - delta)).astype(jnp.bfloat16)
    dv = mm(p.astype(jnp.bfloat16), do_nat)
    dk = mm(ds, q_nat)
    dq = mm(kT_c, ds)
    return dq, dk, dv


def near_bwd_kernel(scal, q_ref, k_ref, v_ref, do_ref, o_ref, l_ref, dq0_ref, dq_ref, dk_ref, dv_ref, k_nat, v_nat, dk_acc, dv_acc):
    head, qb = pl.program_id(0), pl.program_id(1)
    par = scal[4 + head]
    far = qb // 2 == par

    @pl.when(qb == 0)
    def _():
        k_nat[...] = flip(k_ref[...])
        v_nat[...] = flip(v_ref[...])
        dk_acc[...] = jnp.zeros_like(dk_acc)
        dv_acc[...] = jnp.zeros_like(dv_acc)

    def body(masked):
        q = q_ref[...]
        do = do_ref[...]
        q_nat, do_nat = flip(q), flip(do)
        delta = jnp.sum(do.astype(jnp.float32) * o_ref[...].astype(jnp.float32), axis=0, keepdims=True)
        limit = query_limit(scal, qb)
        dq = jnp.where(far, dq0_ref[...], 0.0)
        for c in range(4):
            rows = slice(c * 512, c * 512 + 512)
            twice = jnp.where(far & (par == c // 2), LOG2, 0.0)
            masking = (lambda s: shut(s, scal, scal[1], c % 2, c // 2, limit)) if masked else None
            gq, gk, gv = back_chunk(
                masking, k_nat[rows], v_nat[rows], k_ref[:, rows], q, q_nat, do, do_nat, l_ref[0] - twice, delta
            )
            dq = dq + gq
            dk_acc[rows] += gk
            dv_acc[rows] += gv
        dq_ref[...] = (dq * 0.125).astype(jnp.bfloat16)

    need = scal[2] < scal[1] + 2048
    pl.when(need)(lambda: body(True))
    pl.when(jnp.logical_not(need))(lambda: body(False))

    @pl.when(qb == 3)
    def _():
        dk_ref[...] = dk_acc[...].T
        dv_ref[...] = dv_acc[...].T


def far_block(i, par):
    return jnp.clip(i - 2 * par, 0, 1)


def near_bwd(scal, q, k, v, do, o, l, dq0):
    full = pl.BlockSpec((64, 2048), lambda h, i, s: (h, 0))
    part = pl.BlockSpec((64, QB), lambda h, i, s: (h, i))
    return pl.pallas_call(
        near_bwd_kernel,
        grid_spec=pltpu.PrefetchScalarGridSpec(
            num_scalar_prefetch=1,
            grid=(3, 4),
            in_specs=[
                part,
                full,
                full,
                part,
                part,
                pl.BlockSpec((1, 1, QB), lambda h, i, s: (h, 0, i)),
                pl.BlockSpec((64, QB), lambda h, i, s: (h, far_block(i, s[4 + h]))),
            ],
            out_specs=[part, full, full],
            scratch_shapes=[
                pltpu.VMEM((2048, 64), jnp.bfloat16),
                pltpu.VMEM((2048, 64), jnp.bfloat16),
                pltpu.VMEM((2048, 64), jnp.float32),
                pltpu.VMEM((2048, 64), jnp.float32),
            ],
        ),
        out_shape=[
            jax.ShapeDtypeStruct((192, 2048), jnp.bfloat16),
            jax.ShapeDtypeStruct((192, 2048), jnp.float32),
            jax.ShapeDtypeStruct((192, 2048), jnp.float32),
        ],
        cost_estimate=pl.CostEstimate(flops=32000000000, bytes_accessed=8000000, transcendentals=12582912),
        name="near_bwd",
    )(scal, q, k, v, do, o, l, dq0)


def cross_bwd_kernel(scal, q_ref, k_ref, v_ref, do_ref, o_ref, l_ref, dq_ref, dk_ref, dv_ref, k_nat, v_nat, dk_acc, dv_acc):
    head, i = pl.program_id(0), pl.program_id(1)
    par = scal[4 + head]

    @pl.when(i == 0)
    def _():
        k_nat[...] = flip(k_ref[...])
        v_nat[...] = flip(v_ref[...])
        dk_acc[...] = jnp.zeros_like(dk_acc)
        dv_acc[...] = jnp.zeros_like(dv_acc)

    def body(masked):
        q = q_ref[...]
        do = do_ref[...]
        q_nat, do_nat = flip(q), flip(do)
        delta = jnp.sum(do.astype(jnp.float32) * o_ref[...].astype(jnp.float32), axis=0, keepdims=True)
        limit = query_limit(scal, i + 2 * par)
        dq = None
        for c in range(2):
            rows = slice(c * 512, c * 512 + 512)
            masking = (lambda s: shut(s, scal, scal[3], c, par, limit)) if masked else None
            gq, gk, gv = back_chunk(
                masking, k_nat[rows], v_nat[rows], k_ref[:, rows], q, q_nat, do, do_nat, l_ref[0], delta
            )
            dq = gq if c == 0 else dq + gq
            dk_acc[rows] += gk
            dv_acc[rows] += gv
        dq_ref[...] = dq

    need = scal[3] > scal[1]
    pl.when(need)(lambda: body(True))
    pl.when(jnp.logical_not(need))(lambda: body(False))

    @pl.when(i == 1)
    def _():
        dk_ref[...] = dk_acc[...].T.astype(jnp.bfloat16)
        dv_ref[...] = dv_acc[...].T.astype(jnp.bfloat16)


def cross_bwd(scal, q, kv, do, o, l):
    part = pl.BlockSpec((64, QB), lambda h, i, s: (h, i + 2 * s[4 + h]))
    full = pl.BlockSpec((64, 1024), lambda h, i, s: (h, 0))
    return pl.pallas_call(
        cross_bwd_kernel,
        grid_spec=pltpu.PrefetchScalarGridSpec(
            num_scalar_prefetch=1,
            grid=(3, 2),
            in_specs=[
                part,
                full,
                pl.BlockSpec((64, 1024), lambda h, i, s: (h + 3, 0)),
                part,
                part,
                pl.BlockSpec((1, 1, QB), lambda h, i, s: (h, 0, i + 2 * s[4 + h])),
            ],
            out_specs=[pl.BlockSpec((64, QB), lambda h, i, s: (h, i)), full, full],
            scratch_shapes=[
                pltpu.VMEM((1024, 64), jnp.bfloat16),
                pltpu.VMEM((1024, 64), jnp.bfloat16),
                pltpu.VMEM((1024, 64), jnp.float32),
                pltpu.VMEM((1024, 64), jnp.float32),
            ],
        ),
        out_shape=[
            jax.ShapeDtypeStruct((192, 1024), jnp.float32),
            jax.ShapeDtypeStruct((192, 1024), jnp.bfloat16),
            jax.ShapeDtypeStruct((192, 1024), jnp.bfloat16),
        ],
        cost_estimate=pl.CostEstimate(flops=8000000000, bytes_accessed=6000000, transcendentals=3145728),
        name="cross_bwd",
    )(scal, q, kv, kv, do, o, l)


def contract(left_side, right_side, left_dim, right_dim):
    return lax.dot_general(
        left_side,
        right_side,
        (((left_dim,), (right_dim,)), ((), ())),
        preferred_element_type=jnp.float32,
    )


def swap(value, axis, mask):
    pairs = [(source, source ^ mask) for source in range(lax.axis_size(axis))]
    return lax.ppermute(value, axis, pairs)


def assemble_kernel(where_ref, *refs):
    pieces, full_ref, rows_ref = refs[:-2], refs[-2], refs[-1]
    rows = full_ref.shape[0] // len(pieces)
    for k, piece in enumerate(pieces):
        owner = where_ref[0] ^ k
        full_ref[pl.ds(pl.multiple_of(owner * rows, rows), rows), :] = piece[0:rows, :]
        rows_ref[pl.ds(owner, 1), :] = piece[rows : rows + 1, :].astype(jnp.float32)


def gather_dp(shard, extra, place):
    size = lax.axis_size("dp")
    rows, columns = shard.shape
    if rows % 16:
        return (
            lax.all_gather(shard, "dp", axis=0, tiled=True),
            lax.all_gather(extra, "dp", axis=0, tiled=False).astype(jnp.float32),
        )
    packed = jnp.concatenate((shard, jnp.pad(extra[None, :], ((0, 15), (0, 0)))), axis=0)
    pieces = [packed] + [swap(packed, "dp", mask) for mask in range(1, size)]
    whole = pl.BlockSpec(memory_space=pltpu.VMEM)
    return pl.pallas_call(
        assemble_kernel,
        in_specs=[pl.BlockSpec(memory_space=pltpu.SMEM)] + [whole] * size,
        out_specs=[whole, whole],
        out_shape=[
            jax.ShapeDtypeStruct((size * rows, columns), shard.dtype),
            jax.ShapeDtypeStruct((size, columns), jnp.float32),
        ],
        name="assemble",
    )(place[None], *pieces)


def reduce_dp(values, place):
    size = lax.axis_size("dp")
    rows = values.shape[0] // size
    if size > 8:
        return lax.psum_scatter(values.astype(jnp.float32), "dp", scatter_dimension=0, tiled=True)
    total = lax.dynamic_slice_in_dim(values, place * rows, rows).astype(jnp.float32)
    for mask in range(1, size):
        piece = lax.dynamic_slice_in_dim(values, (place ^ mask) * rows, rows)
        total = total + swap(piece, "dp", mask).astype(jnp.float32)
    return total


def norm_rows(values, axis):
    middle_point = jnp.mean(values, axis=axis, keepdims=True)
    spread = jnp.mean(values * values, axis=axis, keepdims=True) - middle_point * middle_point
    scaling = lax.rsqrt(spread + epsilon)
    return (values - middle_point) * scaling, scaling


def norm_back(grad_hat, normed, scaling, axis):
    return scaling * (
        grad_hat
        - jnp.mean(grad_hat, axis=axis, keepdims=True)
        - normed * jnp.mean(grad_hat * normed, axis=axis, keepdims=True)
    )


def split_parity(rows):
    return rows.reshape(256, 2, -1).transpose(1, 0, 2).reshape(512, -1)


def join_parity(rows):
    return rows.reshape(2, 256, -1).transpose(1, 0, 2).reshape(512, -1)


def halves(value):
    upper = value.astype(jnp.bfloat16)
    return upper, (value - upper.astype(jnp.float32)).astype(jnp.bfloat16)


def local(
    layer_in,
    ln1_gain,
    ln1_bias,
    query_weight,
    query_bias,
    key_weight,
    value_weight,
    value_bias,
    inner_gain,
    inner_bias,
    output_weight,
    output_bias,
    ln2_gain,
    ln2_bias,
    up_weight,
    up_bias,
    outer_gain,
    outer_bias,
    down_weight,
    down_bias,
    out_grad,
    prefix,
):
    size = lax.axis_size("dp")
    place = lax.axis_index("dp")
    member = lax.axis_index("tensor")
    rows = 768 // size
    small = 192 // size
    base = place % 2 * 2048
    prefix_len = lax.dynamic_index_in_dim(prefix, place // 2, keepdims=False)
    parities = [(member * 3 + head) % 2 for head in range(3)]
    scal = jnp.stack([member, base, prefix_len, 2048 - base] + parities).astype(jnp.int32)
    parity_rows = jnp.repeat((member * 3 + jnp.arange(3, dtype=jnp.int32)) % 2, 64)[:, None]

    mine = split_parity(layer_in)
    from_core = swap(mine, "tensor", 1)
    from_chip = swap(mine, "tensor", 2)
    from_both = swap(from_chip, "tensor", 1)
    quarters = (mine, from_core, from_chip, from_both)
    segment = jnp.concatenate([q[:256] for q in quarters] + [q[256:] for q in quarters], axis=0)

    qkv_shard = jnp.concatenate((query_weight, key_weight, value_weight), axis=1)
    qkv_extra = jnp.concatenate((ln1_gain, ln1_bias, query_bias, value_bias))
    qkv_extra = jnp.pad(qkv_extra, (0, 576 - qkv_extra.shape[0]))
    qkv_full, qkv_rows = gather_dp(qkv_shard, qkv_extra, place)
    norm1_scale = qkv_rows[:, :rows].reshape(768)
    norm1_shift = qkv_rows[:, rows : 2 * rows].reshape(768)
    query_shift = qkv_rows[:, 2 * rows : 2 * rows + small].reshape(192)
    value_shift = qkv_rows[:, 2 * rows + small : 2 * rows + 2 * small].reshape(192)

    vectors = jnp.concatenate(
        (output_bias, ln2_gain, ln2_bias, down_bias, up_bias, outer_gain, outer_bias, inner_gain, inner_bias)
    )
    wide_shard = jnp.concatenate((up_weight, down_weight.T, output_weight.T), axis=1)
    wide_shard = jnp.concatenate((wide_shard, jnp.pad(vectors, (0, 1728 - vectors.shape[0]))[None]), axis=0)
    wide_shard = jnp.pad(wide_shard, ((0, -(rows + 1) % 16), (0, 0)))
    wide = lax.all_gather(wide_shard, ("dp", "tensor"), axis=0, tiled=False)
    wide = wide.reshape(size, 4, wide_shard.shape[0], 1728)
    blocks = [lax.dynamic_index_in_dim(wide, member ^ k, axis=1, keepdims=False) for k in range(4)]

    def columns_of(start, stop):
        return jnp.concatenate([b[:, :rows, start:stop].reshape(768, stop - start) for b in blocks], axis=1)

    up_full = columns_of(0, 768)
    down_flip = columns_of(768, 1536)
    output_flip = columns_of(1536, 1728)
    lines = [b[:, rows].astype(jnp.float32) for b in blocks]
    same = lines[0][:, : 4 * rows].reshape(size, 4, rows).transpose(1, 0, 2).reshape(4, 768)
    output_shift, norm2_scale, norm2_shift, down_shift = same[0], same[1], same[2], same[3]
    per_unit = [
        line[:, 4 * rows : 7 * rows].reshape(size, 3, rows).transpose(1, 0, 2).reshape(3, 768) for line in lines
    ]
    units = jnp.concatenate(per_unit, axis=1)
    up_shift, outer_scale, outer_shift = units[0], units[1], units[2]
    per_head = [
        line[:, 7 * rows : 7 * rows + 2 * small].reshape(size, 2, small).transpose(1, 0, 2).reshape(2, 192)
        for line in lines
    ]
    head_rows = jnp.concatenate(per_head, axis=1)
    inner_scale, inner_shift = head_rows[0][:, None], head_rows[1][:, None]

    hat_segment, _ = norm_rows(segment.astype(jnp.float32), 1)
    hidden_one = (hat_segment * norm1_scale + norm1_shift).astype(jnp.bfloat16)
    shifts = jnp.concatenate((query_shift, jnp.zeros(192, jnp.float32), value_shift))[:, None]
    projected = (contract(qkv_full, hidden_one, 0, 1) + shifts).astype(jnp.bfloat16)
    query = projected[:192] * jnp.bfloat16(score_scale)
    key, value = projected[192:384], projected[384:]
    both_rows = jnp.concatenate((parity_rows, parity_rows), axis=0)
    far_own = jnp.where(both_rows == 1, projected[192:, 1024:], projected[192:, :1024])
    far_other = swap(far_own, "dp", 1)
    near_out, near_log = near_fwd(scal, query, key, value)
    attended, log_total = cross_fwd(scal, query, far_other, far_other, near_out, near_log)

    by_row = attended.reshape(192, 2, 4, 256)
    got = swap(by_row[:, :, 2:], "tensor", 2)
    pair = jnp.stack((by_row[:, :, :2], got), axis=0)
    got = swap(pair[:, :, :, 1], "tensor", 1)
    kept = pair[:, :, :, 0]
    heads = jnp.concatenate((kept[0], got[0], kept[1], got[1]), axis=0).reshape(768, 512)

    inner_hat, inner_scaling = norm_rows(heads.astype(jnp.float32), 0)
    inner_rows = (inner_hat * inner_scale + inner_shift).astype(jnp.bfloat16)
    layer_float = mine.astype(jnp.float32)
    middle = layer_float + contract(inner_rows, output_flip, 0, 1) + output_shift
    hat_two, scale_two = norm_rows(middle, 1)
    hidden_two = (hat_two * norm2_scale + norm2_shift).astype(jnp.bfloat16)
    up_rows = jnp.dot(hidden_two, up_full, preferred_element_type=jnp.float32) + up_shift
    activated, gelu_back = jax.vjp(partial(jax.nn.gelu, approximate=False), up_rows)
    outer_hat, outer_scaling = norm_rows(activated, 1)
    outer_rows = (outer_hat * outer_scale + outer_shift).astype(jnp.bfloat16)
    layer_out = middle + contract(outer_rows, down_flip, 1, 1) + down_shift

    grad_low = split_parity(out_grad)
    grad_float = grad_low.astype(jnp.float32)
    grad_down_flip = contract(grad_low, outer_rows, 0, 0)
    outer_grad = jnp.dot(grad_low, down_flip, preferred_element_type=jnp.float32)
    grad_outer_scale = jnp.sum(outer_grad * outer_hat, axis=0)
    grad_outer_shift = jnp.sum(outer_grad, axis=0)
    up_grad = gelu_back(norm_back(outer_grad * outer_scale, outer_hat, outer_scaling, 1))[0].astype(jnp.bfloat16)
    grad_up_shift = jnp.sum(up_grad.astype(jnp.float32), axis=0)
    grad_up = contract(hidden_two, up_grad, 0, 0)
    hidden_two_grad = contract(up_grad, up_full, 1, 1)
    grad_norm2_scale = jnp.sum(hidden_two_grad * hat_two, axis=0)
    grad_norm2_shift = jnp.sum(hidden_two_grad, axis=0)
    middle_grad = grad_float + norm_back(hidden_two_grad * norm2_scale, hat_two, scale_two, 1)
    middle_low = middle_grad.astype(jnp.bfloat16)
    grad_output_shift = jnp.sum(middle_low.astype(jnp.float32), axis=0)
    grad_down_shift = jnp.sum(grad_float, axis=0)
    grad_output_flip = contract(middle_low, inner_rows, 0, 1)
    inner_grad = contract(output_flip, middle_low, 0, 1)
    grad_inner_scale = jnp.sum(inner_grad * inner_hat, axis=1)
    grad_inner_shift = jnp.sum(inner_grad, axis=1)
    heads_grad = norm_back(inner_grad * inner_scale, inner_hat, inner_scaling, 0).astype(jnp.bfloat16)

    split = heads_grad.reshape(4, 192, 2, 256)
    got = swap(jnp.stack((split[1], split[3])), "tensor", 1)
    sent = jnp.stack((split[2], got[1]), axis=2)
    got_chip = swap(sent, "tensor", 2)
    attended_grad = jnp.concatenate(
        (jnp.stack((split[0], got[0]), axis=2), got_chip), axis=2
    ).reshape(192, 2048)

    query_first, far_key_grad, far_value_grad = cross_bwd(scal, query, far_other, attended_grad, attended, log_total)
    returned = swap(jnp.concatenate((far_key_grad, far_value_grad), axis=0), "dp", 1)
    query_low, key_near, value_near = near_bwd(
        scal, query, key, value, attended_grad, attended, log_total, query_first
    )
    side = (jnp.arange(2, dtype=jnp.int32)[None, :] == both_rows)[:, :, None]
    spread_far = jnp.where(side, returned.astype(jnp.float32)[:, None, :], 0.0).reshape(384, 2048)
    key_value_low = (jnp.concatenate((key_near, value_near), axis=0) + spread_far).astype(jnp.bfloat16)
    all_low = jnp.concatenate((query_low, key_value_low), axis=0)
    column_sums = jnp.sum(all_low.astype(jnp.float32), axis=1)

    def pad_small(vector):
        return jnp.pad(vector.reshape(4, size, small), ((0, 0), (0, 0), (0, rows - small))).reshape(4, 768)

    repeated = jnp.stack((grad_output_shift, grad_norm2_scale, grad_norm2_shift, grad_down_shift))
    unit_columns = jnp.stack((grad_up_shift, grad_outer_scale, grad_outer_shift)).reshape(3, 4, 768)
    head_columns = jnp.stack((pad_small(grad_inner_scale), pad_small(grad_inner_shift)))
    extra = jnp.concatenate((jnp.broadcast_to(repeated[:, None], (4, 4, 768)), unit_columns, head_columns), axis=0)
    extra = jnp.pad(extra.transpose(1, 2, 0), ((0, 0), (0, 0), (0, 55))).astype(jnp.bfloat16)

    def wide_block(k):
        return jnp.concatenate(
            (
                grad_up[:, k * 768 : k * 768 + 768].astype(jnp.bfloat16),
                grad_down_flip[:, k * 768 : k * 768 + 768].astype(jnp.bfloat16),
                grad_output_flip[:, k * 192 : k * 192 + 192].astype(jnp.bfloat16),
                extra[k],
            ),
            axis=1,
        )

    got_first = swap(wide_block(3), "tensor", 1)
    got_second = swap(wide_block(1), "tensor", 1)
    to_chip = (wide_block(2).astype(jnp.float32) + got_first.astype(jnp.float32)).astype(jnp.bfloat16)
    from_other = swap(to_chip, "tensor", 2)
    wide_sum = (
        wide_block(0).astype(jnp.float32) + got_second.astype(jnp.float32) + from_other.astype(jnp.float32)
    ).astype(jnp.bfloat16)
    wide_own = reduce_dp(wide_sum, place)

    partial_rows = contract(all_low, qkv_full, 0, 1).reshape(2, 4, 256, 768)
    got = swap(jnp.stack((partial_rows[:, 1], partial_rows[:, 3])).astype(jnp.bfloat16), "tensor", 1)
    got = got.astype(jnp.float32)
    got_chip = swap((partial_rows[:, 2] + got[1]).astype(jnp.bfloat16), "tensor", 2)
    hidden_one_grad = (partial_rows[:, 0] + got[0] + got_chip.astype(jnp.float32)).reshape(512, 768)

    grad_qkv = contract(hidden_one, all_low, 0, 1)
    full_float = qkv_full.astype(jnp.float32)
    along = jnp.sum(full_float * grad_qkv, axis=1)
    shift_part = jnp.sum(full_float * column_sums[None, :], axis=1)

    def small_column(vector):
        return jnp.pad(vector.reshape(size, small), ((0, 0), (0, rows - small))).reshape(768)

    columns = [*halves(along), *halves(shift_part)]
    columns += [*halves(small_column(column_sums[:192])), *halves(small_column(column_sums[384:]))]
    qkv_grads = jnp.concatenate(
        (grad_qkv.astype(jnp.bfloat16), jnp.pad(jnp.stack(columns, axis=1), ((0, 0), (0, 56)))), axis=1
    )
    qkv_own = reduce_dp(qkv_grads, place)
    norm_pair = jnp.stack((qkv_own[:, 576] + qkv_own[:, 577], qkv_own[:, 578] + qkv_own[:, 579]))
    norm_pair = norm_pair + swap(norm_pair, "tensor", 1)
    norm_pair = norm_pair + swap(norm_pair, "tensor", 2)
    gain_own, bias_own = ln1_gain.astype(jnp.float32), ln1_bias.astype(jnp.float32)
    grad_ln1_gain = (norm_pair[0] - bias_own * norm_pair[1]) / gain_own

    hat_one, scale_one = norm_rows(layer_float, 1)
    input_grad = middle_grad + norm_back(hidden_one_grad * norm1_scale, hat_one, scale_one, 1)

    return (
        join_parity(layer_out.astype(jnp.bfloat16)),
        join_parity(input_grad),
        grad_ln1_gain,
        norm_pair[1],
        qkv_own[:, :192],
        qkv_own[:small, 580] + qkv_own[:small, 581],
        qkv_own[:, 192:384],
        qkv_own[:, 384:576],
        qkv_own[:small, 582] + qkv_own[:small, 583],
        wide_own[:small, 1735],
        wide_own[:small, 1736],
        wide_own[:, 1536:1728].T,
        wide_own[:, 1728],
        wide_own[:, 1729],
        wide_own[:, 1730],
        wide_own[:, :768],
        wide_own[:, 1732],
        wide_own[:, 1733],
        wide_own[:, 1734],
        wide_own[:, 768:1536].T,
        wide_own[:, 1731],
    )


def solution(mesh):
    in_specs = (
        P(("dp", "tensor"), None),
        P("dp"),
        P("dp"),
        P("dp", "tensor"),
        P(("tensor", "dp")),
        P("dp", "tensor"),
        P("dp", "tensor"),
        P(("tensor", "dp")),
        P(("tensor", "dp")),
        P(("tensor", "dp")),
        P("tensor", "dp"),
        P("dp"),
        P("dp"),
        P("dp"),
        P("dp", "tensor"),
        P(("tensor", "dp")),
        P(("tensor", "dp")),
        P(("tensor", "dp")),
        P("tensor", "dp"),
        P("dp"),
        P(("dp", "tensor"), None),
        P(),
    )
    out_specs = (
        P(("dp", "tensor"), None),
        P(("dp", "tensor"), None),
        P("dp"),
        P("dp"),
        P("dp", "tensor"),
        P(("tensor", "dp")),
        P("dp", "tensor"),
        P("dp", "tensor"),
        P(("tensor", "dp")),
        P(("tensor", "dp")),
        P(("tensor", "dp")),
        P("tensor", "dp"),
        P("dp"),
        P("dp"),
        P("dp"),
        P("dp", "tensor"),
        P(("tensor", "dp")),
        P(("tensor", "dp")),
        P(("tensor", "dp")),
        P("tensor", "dp"),
        P("dp"),
    )
    return jax.shard_map(local, mesh=mesh, in_specs=in_specs, out_specs=out_specs, check_vma=False)
```
